32 devices in a mesh: grp: 8 (over z, y), fsdp: 4 (over x, core).
Axes of the slice: x: 2, y: 2, z: 4, core: 2. Of those that a mesh axis runs over, the one named last changes fastest.
Arguments:
- code_ids: int32 [128, 256], P(('grp', 'fsdp')), may hold values from 0 to 1023
- mask_pos: int32 [128, 128], P(('grp', 'fsdp')), may hold values from 0 to 255, as said below
- mask_count: int32 [128], P(('grp', 'fsdp')), may hold values from 1 to 128, as said below
- block_order: int32 [48], replicated, may hold values from 0 to 47, each once
- step_count: int32 [], replicated, may hold values from 1 to 20
- blocks: float32 [48, 384, 384], P(None, 'fsdp')
- block_mom: float32 [48, 384, 384], P('fsdp'), may hold values from -6.1035156e-05 to 6.1035156e-05
- block_var: float32 [48, 384, 384], P('fsdp'), may hold values from 2e-12 to 2e-11
- rot_bases: float32 [48, 2, 384, 384], P('fsdp'), as said below
- embedding: float32 [2025, 768], P(None, 'fsdp'), may hold values from -0.4375 to 0.4375
- embed_mom: float32 [2025, 768], P(None, 'fsdp'), may hold values from -6.1035156e-05 to 6.1035156e-05
- embed_var: float32 [2025, 768], P(None, 'fsdp'), may hold values from 2e-12 to 2e-11
- position: float32 [256, 768], P(None, 'fsdp'), may hold values from -0.4375 to 0.4375
- pos_mom: float32 [256, 768], P(None, 'fsdp'), may hold values from -6.1035156e-05 to 6.1035156e-05
- pos_var: float32 [256, 768], P(None, 'fsdp'), may hold values from 2e-12 to 2e-11
- head_w: float32 [768, 768], P(None, 'fsdp'), may hold values from -0.21875 to 0.21875
- head_mom: float32 [768, 768], P(None, 'fsdp'), may hold values from -6.1035156e-05 to 6.1035156e-05
- head_var: float32 [768, 768], P(None, 'fsdp'), may hold values from 2e-12 to 2e-11
- vectors: float32 [17, 768], P(None, 'fsdp'), may hold values from -1.25 to 1.25
- vec_mom: float32 [17, 768], P(None, 'fsdp'), may hold values from -6.1035156e-05 to 6.1035156e-05
- vec_var: float32 [17, 768], P(None, 'fsdp'), may hold values from 2e-12 to 2e-11
- out_bias: float32 [2025], replicated, may hold values from -3 to 3
- bias_mom: float32 [2025], replicated, may hold values from -6.1035156e-05 to 6.1035156e-05
- bias_var: float32 [2025], replicated, may hold values from 2e-12 to 2e-11
Outputs:
- loss_out: float32 [], replicated
- clip_norm: float32 [], replicated
- new_blocks: float32 [48, 384, 384], P(None, 'fsdp')
- new_block_mom: float32 [48, 384, 384], P('fsdp')
- new_block_var: float32 [48, 384, 384], P('fsdp')
- new_embedding: float32 [2025, 768], P(None, 'fsdp')
- new_embed_mom: float32 [2025, 768], P(None, 'fsdp')
- new_embed_var: float32 [2025, 768], P(None, 'fsdp')
- new_position: float32 [256, 768], P(None, 'fsdp')
- new_pos_mom: float32 [256, 768], P(None, 'fsdp')
- new_pos_var: float32 [256, 768], P(None, 'fsdp')
- new_head_w: float32 [768, 768], P(None, 'fsdp')
- new_head_mom: float32 [768, 768], P(None, 'fsdp')
- new_head_var: float32 [768, 768], P(None, 'fsdp')
- new_vectors: float32 [17, 768], P(None, 'fsdp')
- new_vec_mom: float32 [17, 768], P(None, 'fsdp')
- new_vec_var: float32 [17, 768], P(None, 'fsdp')
- new_out_bias: float32 [2025], replicated
- new_bias_mom: float32 [2025], replicated
- new_bias_var: float32 [2025], replicated
The draws below stay inside these ranges and needn't reach their ends.
Inputs may be any that keep to these rules, and one draw needn't show every extreme that they name: `mask_pos`: each row holds 128 different positions. `mask_count`: the largest count is exactly 128. `block_order`: each number once. Each of the matrices rot_bases[s, 0] and rot_bases[s, 1] is orthogonal.
All inputs are finite; a program needn't handle non-finite values.
Results may differ from the reference program's by a relative error of at most 0.002.
The reference program's roundings to bfloat16 on the way count: a program that leaves them out, or rounds other values in their place, can miss the bound.
Values may be sent and summed in bfloat16 or wider, within the bound.
No kernel may reach another device: no remote copies, remote signals or barrier semaphores. Data moves between devices by JAX's collectives and lax.ppermute only.
A program may use at most 640 MiB of HBM per device.

```python
import math
import jax
import jax.numpy as jnp
from jax import lax

D = 768
HEADS = 16
HD = 48
FF = 3072
VOCAB = 2025
CODES = 1024
SEQ = 256
BS = 384
MASKN = 128
NB = 48
NVEC = 17
SEQS = 128


def draw_mask_pos(key, part):
    scores = jax.random.randint(key, (SEQS, SEQ), 0, SEQ) * SEQ + jnp.arange(SEQ, dtype=jnp.int32)[None, :]
    order = jnp.argsort(scores, axis=1, stable=True)
    return order[:, :MASKN].astype(jnp.int32)


def draw_mask_count(key, part):
    counts = jax.random.randint(key, (SEQS,), 1, MASKN + 1)
    return counts.at[0].set(MASKN).astype(jnp.int32)


def draw_blocks(key, part):
    base = jax.random.normal(key, (NB, BS, BS), jnp.float32)
    square = D // BS * (D // BS)
    wide = D // BS * (FF // BS)
    index = jnp.arange(NB)
    factor = jnp.where(index < 3 * square, D ** (-0.5), jnp.where(index < 4 * square, 8.0 * D ** (-0.5), jnp.where(index < 4 * square + wide, D ** (-0.5), 1.5 * FF ** (-0.5))))
    return (base * factor[:, None, None]).astype(jnp.float32)


def draw_rot_bases(key, part):
    base = jax.random.normal(key, (NB, 2, BS, BS), jnp.float32)
    factor_q, factor_r = jnp.linalg.qr(base)
    return factor_q.astype(jnp.float32)


def plant(entries, own_key, low, top_value):
    longest = entries.shape.index(max(entries.shape))
    spots = []
    for shift in (0, 1):
        where = [jax.random.randint(jax.random.fold_in(own_key, axis), (), 0, length) for axis, length in enumerate(entries.shape)]
        where[longest] = (where[longest] + shift) % entries.shape[longest]
        spots.append(tuple(where))
    return entries.at[spots[0]].set(low).at[spots[1]].set(top_value)


def block_scale(rng, shape, shards, smallest, high):
    gain, own = 1.0, jax.random.fold_in(rng, 6)
    for axis_at, blocks in shards:
        heights = jnp.exp(jax.random.uniform(jax.random.fold_in(own, axis_at), (blocks,), jnp.float32, smallest / len(shards), high / len(shards)))
        gain = gain * jnp.repeat(heights, shape[axis_at] // blocks).reshape([-1 if axis == axis_at else 1 for axis in range(len(shape))])
    return gain


def noise(rng, dims, scale, bound, shards=(), kind=jnp.bfloat16):
    values = jax.random.normal(rng, dims, jnp.float32) * scale
    if len(shards) > 0:
        values = block_scale(rng, dims, shards, -0.22, 0.18) * values
    return jnp.clip(values, min=-bound, max=bound).astype(kind)


def setup_inputs(seed: int = 0) -> dict:
    key_of = jax.random.split(jax.random.key(seed), 25)
    code_ids = plant(jax.random.randint(key_of[0], (SEQS, SEQ), 0, CODES), jax.random.fold_in(key_of[0], 1), 0, CODES - 1).astype(jnp.int32)
    mask_pos = draw_mask_pos(jax.random.fold_in(key_of[24], 71), 0)
    mask_count = draw_mask_count(jax.random.fold_in(key_of[24], 71), 0)
    block_order = jax.random.permutation(key_of[3], NB).astype(jnp.int32)
    step_count = jax.random.randint(key_of[4], (), 1, 21).astype(jnp.int32)
    blocks = draw_blocks(jax.random.fold_in(key_of[24], 71), 0)
    block_mom = noise(key_of[6], (NB, BS, BS), (1e-5), 6.103515625e-05, ((0, 4),), jnp.float32)
    block_var = jnp.clip(jnp.exp(math.log(1.9999999920083944e-11) - 2.3025851 * jax.random.uniform(key_of[7], (NB, BS, BS), jnp.float32) ** block_scale(key_of[7], (NB, BS, BS), ((0, 4),), -0.2, 0.2)), 1.9999999920083944e-12, 1.9999999920083944e-11)
    rot_bases = draw_rot_bases(jax.random.fold_in(key_of[24], 71), 0)
    embedding = noise(key_of[9], (VOCAB, D), 0.07, 0.4375, ((1, 4),), jnp.float32)
    embed_mom = noise(key_of[10], (VOCAB, D), (1e-5), 6.103515625e-05, ((1, 4),), jnp.float32)
    embed_var = jnp.clip(jnp.exp(math.log(1.9999999920083944e-11) - 2.3025851 * jax.random.uniform(key_of[11], (VOCAB, D), jnp.float32) ** block_scale(key_of[11], (VOCAB, D), ((1, 4),), -0.2, 0.2)), 1.9999999920083944e-12, 1.9999999920083944e-11)
    position = noise(key_of[12], (SEQ, D), 0.07, 0.4375, ((1, 4),), jnp.float32)
    pos_mom = noise(key_of[13], (SEQ, D), (1e-5), 6.103515625e-05, ((1, 4),), jnp.float32)
    pos_var = jnp.clip(jnp.exp(math.log(1.9999999920083944e-11) - 2.3025851 * jax.random.uniform(key_of[14], (SEQ, D), jnp.float32) ** block_scale(key_of[14], (SEQ, D), ((1, 4),), -0.2, 0.2)), 1.9999999920083944e-12, 1.9999999920083944e-11)
    head_w = noise(key_of[15], (D, D), D ** -0.5, 0.21875, ((1, 4),), jnp.float32)
    head_mom = noise(key_of[16], (D, D), (1e-5), 6.103515625e-05, ((1, 4),), jnp.float32)
    head_var = jnp.clip(jnp.exp(math.log(1.9999999920083944e-11) - 2.3025851 * jax.random.uniform(key_of[17], (D, D), jnp.float32) ** block_scale(key_of[17], (D, D), ((1, 4),), -0.2, 0.2)), 1.9999999920083944e-12, 1.9999999920083944e-11)
    vectors = noise(key_of[18], (NVEC, D), 0.2, 1.25, ((1, 4),), jnp.float32)
    vec_mom = noise(key_of[19], (NVEC, D), (1e-5), 6.103515625e-05, ((1, 4),), jnp.float32)
    vec_var = jnp.clip(jnp.exp(math.log(1.9999999920083944e-11) - 2.3025851 * jax.random.uniform(key_of[20], (NVEC, D), jnp.float32) ** block_scale(key_of[20], (NVEC, D), ((1, 4),), -0.2, 0.2)), 1.9999999920083944e-12, 1.9999999920083944e-11)
    out_bias = noise(key_of[21], (VOCAB,), 0.5, 3.0, (), jnp.float32)
    bias_mom = noise(key_of[22], (VOCAB,), (1e-5), 6.103515625e-05, (), jnp.float32)
    bias_var = jnp.clip(jnp.exp(jax.random.uniform(key_of[23], (VOCAB,), jnp.float32, math.log(1.9999999920083944e-12), math.log(1.9999999920083944e-11))), 1.9999999920083944e-12, 1.9999999920083944e-11)
    return {"code_ids": code_ids, "mask_pos": mask_pos, "mask_count": mask_count, "block_order": block_order, "step_count": step_count, "blocks": blocks, "block_mom": block_mom, "block_var": block_var, "rot_bases": rot_bases, "embedding": embedding, "embed_mom": embed_mom, "embed_var": embed_var, "position": position, "pos_mom": pos_mom, "pos_var": pos_var, "head_w": head_w, "head_mom": head_mom, "head_var": head_var, "vectors": vectors, "vec_mom": vec_mom, "vec_var": vec_var, "out_bias": out_bias, "bias_mom": bias_mom, "bias_var": bias_var}


@jax.custom_vjp
def low(v):
    return lax.optimization_barrier(v.astype(jnp.bfloat16)).astype(jnp.float32)

@jax.custom_vjp
def low_back(v):
    return v

def low_keep(v):
    return (low(v), None)

def low_pass(kept, grad):
    return (grad,)

def back_keep(v):
    return (v, None)

def back_low(kept, grad):
    return (low(grad),)
low.defvjp(low_keep, low_pass)
low_back.defvjp(back_keep, back_low)
BETA_ONE = 0.9
BETA_TWO = 0.999
ADAM_EPS = 1e-08
LEARN_RATE = 0.02
DECAY_RATE = 0.1
CLIP_LEVEL = 0.25
NORM_EPS = 1e-06
TOP_PRECISION = lax.Precision.HIGHEST

def layer_norm(values, scale_gain, offset):
    center = values - lax.optimization_barrier(jnp.mean(values, axis=-1, keepdims=True))
    spread = lax.optimization_barrier(jnp.mean(center * center, axis=-1, keepdims=True))
    return center * lax.rsqrt(spread + NORM_EPS) * scale_gain + offset

def exact_gelu(values):
    return jax.nn.gelu(values, approximate=False)

def block_apply(inputs, weight):
    row_count = inputs.shape[0]
    count_in, count_out, block_size = (weight.shape[0], weight.shape[1], weight.shape[2])
    shaped = inputs.reshape(row_count, count_in, block_size)
    result = jnp.einsum('tir,ijrc->tjc', shaped, weight, precision=TOP_PRECISION)
    return result.reshape(row_count, count_out * block_size)

def split_blocks(stacked):
    per_side = D // BS
    per_wide = FF // BS
    square = per_side * per_side
    w_query = stacked[0:square].reshape(per_side, per_side, BS, BS)
    w_key = stacked[square:2 * square].reshape(per_side, per_side, BS, BS)
    w_value = stacked[2 * square:3 * square].reshape(per_side, per_side, BS, BS)
    w_out = stacked[3 * square:4 * square].reshape(per_side, per_side, BS, BS)
    w_up = stacked[4 * square:4 * square + per_side * per_wide].reshape(per_side, per_wide, BS, BS)
    w_down = stacked[4 * square + per_side * per_wide:].reshape(per_wide, per_side, BS, BS)
    return (w_query, w_key, w_value, w_out, w_up, w_down)

def group_loss(params, code_rows, place_rows, count_rows, masked_total):
    blocks, embedding, position, head_w, vectors, out_bias = params
    score_scale = float(HD) ** (-0.5)
    sent_blocks = low(blocks)
    sent_embed = low(embedding)
    sent_pos = low(position)
    sent_head = low(head_w)
    sent_vec = low(vectors)
    w_query, w_key, w_value, w_out, w_up, w_down = split_blocks(sent_blocks)
    seq_count = code_rows.shape[0]
    row_count = seq_count * SEQ
    slot_index = jnp.arange(MASKN, dtype=jnp.int32)
    valid_slot = slot_index[None, :] < count_rows[:, None]
    is_masked = jnp.any((place_rows[:, :, None] == jnp.arange(SEQ, dtype=jnp.int32)[None, None, :]) & valid_slot[:, :, None], axis=1)
    token_ids = jnp.where(is_masked, VOCAB - 1, code_rows).astype(jnp.int32)
    embedded = (sent_embed[token_ids] + sent_pos[None]).reshape(row_count, D)
    act_a = low(layer_norm(embedded, 1.0 + sent_vec[0], sent_vec[1]))
    query = low(low_back(block_apply(act_a, w_query) + sent_vec[8]))
    keys = low(low_back(block_apply(act_a, w_key)))
    vals = low(low_back(block_apply(act_a, w_value) + sent_vec[9]))
    query_heads = query.reshape(seq_count, SEQ, HEADS, HD)
    key_heads = keys.reshape(seq_count, SEQ, HEADS, HD)
    value_heads = vals.reshape(seq_count, SEQ, HEADS, HD)
    scores = low_back(jnp.einsum('bqhd,bkhd->bhqk', query_heads, key_heads, precision=TOP_PRECISION) * score_scale)
    probabilities = low(jax.nn.softmax(scores, axis=-1))
    mixed = jnp.einsum('bhqk,bkhd->bqhd', probabilities, value_heads, precision=TOP_PRECISION).reshape(row_count, D)
    mixed = low(low_back(mixed))
    resid_one = embedded + low_back(block_apply(mixed, w_out) + sent_vec[10])
    act_m = low(layer_norm(resid_one, 1.0 + sent_vec[2], sent_vec[3]))
    hidden_pre = low_back(block_apply(act_m, w_up) + sent_vec[13:].reshape(FF))
    act_h = low(exact_gelu(hidden_pre))
    resid_two = resid_one + low_back(block_apply(act_h, w_down) + sent_vec[11])
    final_norm = layer_norm(resid_two, 1.0 + sent_vec[4], sent_vec[5]).reshape(seq_count, SEQ, D)
    picked = low(jnp.take_along_axis(final_norm, place_rows[:, :, None], axis=1).reshape(seq_count * MASKN, D))
    head_pre = low_back(jnp.dot(picked, sent_head, precision=TOP_PRECISION) + sent_vec[12])
    act_t = low(layer_norm(exact_gelu(head_pre), 1.0 + sent_vec[6], sent_vec[7]))
    logits = low_back(jnp.dot(act_t, sent_embed.T, precision=TOP_PRECISION) + out_bias)
    targets = jnp.take_along_axis(code_rows, place_rows, axis=1).reshape(-1)
    log_norm = jax.nn.logsumexp(logits, axis=-1)
    picked_logit = jnp.take_along_axis(logits, targets[:, None], axis=1)[:, 0]
    slot_weight = valid_slot.reshape(-1).astype(logits.dtype)
    return jnp.sum(slot_weight * (log_norm - picked_logit)) / masked_total

def adam_moments(gradient, moment, second, corr_one, corr_two):
    new_moment = BETA_ONE * moment + (1.0 - BETA_ONE) * gradient
    new_second = BETA_TWO * second + (1.0 - BETA_TWO) * gradient * gradient
    direction = new_moment / corr_one / (jnp.sqrt(new_second / corr_two) + ADAM_EPS)
    return (new_moment, new_second, direction)

def adamw(weight, gradient, moment, second, corr_one, corr_two, decay):
    new_moment, new_second, direction = adam_moments(gradient, moment, second, corr_one, corr_two)
    return (weight - LEARN_RATE * (direction + decay * weight), new_moment, new_second)

def reference(code_ids, mask_pos, mask_count, block_order, step_count, blocks, block_mom, block_var, rot_bases, embedding, embed_mom, embed_var, position, pos_mom, pos_var, head_w, head_mom, head_var, vectors, vec_mom, vec_var, out_bias, bias_mom, bias_var):
    masked_total = jnp.sum(mask_count).astype(jnp.float32)
    group_size = math.gcd(SEQS, max(1, 4096 // SEQ))
    count_groups = SEQS // group_size
    params = (blocks, embedding, position, head_w, vectors, out_bias)
    scanned = (code_ids.reshape(count_groups, group_size, SEQ), mask_pos.reshape(count_groups, group_size, MASKN), mask_count.reshape(count_groups, group_size))

    def scan_step(running, inputs):
        code_rows, place_rows, count_rows = inputs

        def loss_of(*weights):
            return group_loss(weights, code_rows, place_rows, count_rows, masked_total)
        loss_value, pullback = jax.vjp(loss_of, *params)
        gradients = pullback(jnp.ones_like(loss_value))
        return ((running[0] + loss_value, jax.tree.map(jnp.add, running[1], tuple(gradients))), None)
    initial = (jnp.zeros_like(masked_total), jax.tree.map(jnp.zeros_like, params))
    (loss_sum, gradients), _ = lax.scan(scan_step, initial, scanned)
    grad_blocks, grad_embed, grad_pos, grad_head, grad_vec, grad_bias = gradients
    square_sum = grad_blocks.sum() * 0.0
    for item in gradients:
        square_sum = square_sum + jnp.sum(item * item)
    clip_norm = jnp.sqrt(square_sum)
    clip_scale = CLIP_LEVEL / jnp.maximum(clip_norm, CLIP_LEVEL)
    step_float = step_count.astype(jnp.float32)
    corr_one = 1.0 - jnp.power(BETA_ONE, step_float)
    corr_two = 1.0 - jnp.power(BETA_TWO, step_float)
    slot_grads = jnp.take(grad_blocks, block_order, axis=0) * clip_scale
    left_basis = rot_bases[:, 0]
    right_basis = rot_bases[:, 1]
    rotated = jnp.einsum('sji,sjk->sik', left_basis, slot_grads, precision=TOP_PRECISION)
    rotated = jnp.einsum('sik,skl->sil', rotated, right_basis, precision=TOP_PRECISION)
    new_block_mom, new_block_var, direction = adam_moments(rotated, block_mom, block_var, corr_one, corr_two)
    turned = jnp.einsum('sij,sjk->sik', left_basis, direction, precision=TOP_PRECISION)
    slot_update = jnp.einsum('sik,slk->sil', turned, right_basis, precision=TOP_PRECISION)
    update = jnp.zeros_like(blocks).at[block_order].set(slot_update)
    new_blocks = blocks - LEARN_RATE * (update + DECAY_RATE * blocks)
    new_embedding, new_embed_mom, new_embed_var = adamw(embedding, grad_embed * clip_scale, embed_mom, embed_var, corr_one, corr_two, DECAY_RATE)
    new_position, new_pos_mom, new_pos_var = adamw(position, grad_pos * clip_scale, pos_mom, pos_var, corr_one, corr_two, DECAY_RATE)
    new_head_w, new_head_mom, new_head_var = adamw(head_w, grad_head * clip_scale, head_mom, head_var, corr_one, corr_two, DECAY_RATE)
    new_vectors, new_vec_mom, new_vec_var = adamw(vectors, grad_vec * clip_scale, vec_mom, vec_var, corr_one, corr_two, 0.0)
    new_out_bias, new_bias_mom, new_bias_var = adamw(out_bias, grad_bias * clip_scale, bias_mom, bias_var, corr_one, corr_two, 0.0)
    return (loss_sum, clip_norm, new_blocks, new_block_mom, new_block_var, new_embedding, new_embed_mom, new_embed_var, new_position, new_pos_mom, new_pos_var, new_head_w, new_head_mom, new_head_var, new_vectors, new_vec_mom, new_vec_var, new_out_bias, new_bias_mom, new_bias_var)
```

```python
import jax
import jax.numpy as jnp
from jax import lax
from jax.experimental import pallas as pl
from jax.experimental.pallas import tpu as pltpu
from jax.sharding import PartitionSpec as P

D = 768
HEADS = 16
HD = 48
FF = 3072
VOCAB = 2025
VPAD = 2048
CODES = 1024
SEQ = 256
BS = 384
MASKN = 128
NB = 48
NVEC = 17
SIDE = D // BS
WIDE = FF // BS
SQ = SIDE * SIDE

BETA_ONE = 0.9
BETA_TWO = 0.999
ADAM_EPS = 1e-08
LEARN_RATE = 0.02
DECAY_RATE = 0.1
CLIP_LEVEL = 0.25
NORM_EPS = 1e-06
SEND_TOP = 14.0
CLIP_UP = float(2**17)
ROOT_HALF = 0.7071067811865476
PDF_FACTOR = 0.3989422804014327
F32 = jnp.float32
BF = jnp.bfloat16
F16 = jnp.float16


def mm(a, b, ca=1, cb=0):
    return lax.dot_general(a, b, (((ca,), (cb,)), ((), ())), preferred_element_type=F32)


def head_window(head):
    low = head * HD
    start = low // 128 * 128
    width = 128 if low + HD <= start + 128 else 256
    return low, start, width


def lane_mask(low, start, width):
    lane = lax.broadcasted_iota(jnp.int32, (1, width), 1) + start
    return (lane >= low) & (lane < low + HD)


def softmax_rows(q, k):
    scores = mm(q, k, 1, 1) * (HD**-0.5)
    top = jnp.max(scores, axis=1, keepdims=True)
    parts = jnp.exp(scores - top)
    return parts * (1.0 / jnp.sum(parts, axis=1, keepdims=True))


def attn_fwd_kernel(qkv_ref, o_ref, acc_ref):
    acc_ref[...] = jnp.zeros_like(acc_ref)
    for head in range(HEADS):
        low, start, width = head_window(head)
        keep = lane_mask(low, start, width)
        q = qkv_ref[:, pl.ds(start, width)]
        k = qkv_ref[:, pl.ds(D + start, width)]
        v = qkv_ref[:, pl.ds(2 * D + start, width)]
        q = jnp.where(keep, q, jnp.zeros_like(q))
        v = jnp.where(keep, v, jnp.zeros_like(v))
        probs = softmax_rows(q, k).astype(BF)
        acc_ref[:, pl.ds(start, width)] += mm(probs, v)
    o_ref[...] = acc_ref[...].astype(BF)


def attn_bwd_kernel(qkv_ref, do_ref, out_ref, acc_ref):
    acc_ref[...] = jnp.zeros_like(acc_ref)
    for head in range(HEADS):
        low, start, width = head_window(head)
        keep = lane_mask(low, start, width)
        q = qkv_ref[:, pl.ds(start, width)]
        k = qkv_ref[:, pl.ds(D + start, width)]
        v = qkv_ref[:, pl.ds(2 * D + start, width)]
        do = do_ref[:, pl.ds(start, width)]
        q = jnp.where(keep, q, jnp.zeros_like(q))
        do = jnp.where(keep, do, jnp.zeros_like(do))
        probs = softmax_rows(q, k)
        k = jnp.where(keep, k, jnp.zeros_like(k))
        dp = mm(do, v, 1, 1)
        ds = (probs * (dp - jnp.sum(dp * probs, axis=1, keepdims=True))).astype(BF)
        acc_ref[:, pl.ds(start, width)] += mm(ds, k)
        acc_ref[:, pl.ds(D + start, width)] += mm(ds, q, 0, 0)
        acc_ref[:, pl.ds(2 * D + start, width)] += mm(probs.astype(BF), do, 0, 0)
    out_ref[:, : 2 * D] = (acc_ref[:, : 2 * D] * (HD**-0.5)).astype(BF)
    out_ref[:, 2 * D :] = acc_ref[:, 2 * D :].astype(BF)


def attn_fwd(qkv):
    rows = qkv.shape[0]
    return pl.pallas_call(
        attn_fwd_kernel,
        grid=(rows // SEQ,),
        in_specs=[pl.BlockSpec((SEQ, 3 * D), lambda s: (s, 0))],
        out_specs=pl.BlockSpec((SEQ, D), lambda s: (s, 0)),
        out_shape=jax.ShapeDtypeStruct((rows, D), BF),
        scratch_shapes=[pltpu.VMEM((SEQ, D), F32)],
        cost_estimate=pl.CostEstimate(
            flops=rows * SEQ * D * 4 * 4, transcendentals=rows * SEQ * HEADS, bytes_accessed=rows * D * 8
        ),
        name="attn_fwd",
    )(qkv)


def attn_bwd(qkv, do):
    rows = qkv.shape[0]
    return pl.pallas_call(
        attn_bwd_kernel,
        grid=(rows // SEQ,),
        in_specs=[
            pl.BlockSpec((SEQ, 3 * D), lambda s: (s, 0)),
            pl.BlockSpec((SEQ, D), lambda s: (s, 0)),
        ],
        out_specs=pl.BlockSpec((SEQ, 3 * D), lambda s: (s, 0)),
        out_shape=jax.ShapeDtypeStruct((rows, 3 * D), BF),
        scratch_shapes=[pltpu.VMEM((SEQ, 3 * D), F32)],
        cost_estimate=pl.CostEstimate(
            flops=rows * SEQ * D * 4 * 10, transcendentals=rows * SEQ * HEADS, bytes_accessed=rows * D * 14
        ),
        name="attn_bwd",
    )(qkv, do)


def norm_parts(x):
    center = x - jnp.mean(x, axis=-1, keepdims=True)
    rstd = lax.rsqrt(jnp.mean(center * center, axis=-1, keepdims=True) + NORM_EPS)
    return center * rstd, rstd


def norm_back(dy, xhat, rstd, gain):
    dxhat = dy * gain
    inner = dxhat - jnp.mean(dxhat, axis=-1, keepdims=True)
    inner = inner - xhat * jnp.mean(dxhat * xhat, axis=-1, keepdims=True)
    return inner * rstd, jnp.sum(dy * xhat, axis=0), jnp.sum(dy, axis=0)


def gelu_cdf(u):
    return 0.5 * (1.0 + lax.erf(u * ROOT_HALF))


def gelu_grad(u):
    return gelu_cdf(u) + u * (PDF_FACTOR * jnp.exp(-0.5 * u * u))


def col_total(values):
    return jnp.sum(values.astype(F32), axis=0)


def swap(values, axis, size, bit):
    return lax.ppermute(values, axis, [(i, i ^ bit) for i in range(size)])


def bound_exponent(bound):
    return jnp.ceil(jnp.log2(jnp.maximum(bound, 1e-30))) + 1.0


def pack(values, exponent):
    lanes = values.shape[-1]
    scaled = (values * jnp.exp2(SEND_TOP - exponent)).astype(F16).reshape(-1, lanes)
    return jnp.concatenate([scaled, jnp.full((8, lanes), exponent, F32).astype(F16)], axis=0)


def unpack(packed, shape):
    exponent = packed[-1, 0].astype(F32)
    values = packed[:-8].astype(F32) * jnp.exp2(exponent - SEND_TOP)
    return values.reshape(shape), jnp.exp2(exponent)


def reduce_chunk(values, sizes, index):
    parts, shards, rows, lanes = values.shape
    size_f, size_g = sizes
    index_f, index_g = index
    bound = jnp.max(jnp.abs(values))
    bit = 1
    while bit < size_f:
        shards = shards // 2
        both = values.reshape(parts, shards, 2, rows, lanes)
        mine = (index_f // bit) % 2
        keep = lax.dynamic_index_in_dim(both, mine, 2, keepdims=False)
        send = lax.dynamic_index_in_dim(both, 1 - mine, 2, keepdims=False)
        got, other = unpack(swap(pack(send, bound_exponent(bound)), "fsdp", size_f, bit), keep.shape)
        values = keep + got
        bound = bound + other
        bit *= 2
    values = values.reshape(parts, rows, lanes)
    bit = 1
    while bit < size_g // 2:
        rows = rows // 2
        both = values.reshape(parts, 2, rows, lanes)
        mine = (index_g // bit) % 2
        keep = lax.dynamic_index_in_dim(both, mine, 1, keepdims=False)
        send = lax.dynamic_index_in_dim(both, 1 - mine, 1, keepdims=False)
        got, other = unpack(swap(pack(send, bound_exponent(bound)), "grp", size_g, bit), keep.shape)
        values = keep + got
        bound = bound + other
        bit *= 2
    packed = pack(values, bound_exponent(bound))
    mine = unpack(packed, values.shape)[0]
    return mine + unpack(swap(packed, "grp", size_g, bit), values.shape)[0]


def gather_rows(piece, size_g, index_g):
    bit = size_g // 4
    while bit >= 1:
        other = swap(piece, "grp", size_g, bit)
        first = (index_g // bit) % 2 == 0
        piece = jnp.concatenate([jnp.where(first, piece, other), jnp.where(first, other, piece)], axis=1)
        bit //= 2
    return piece


def adam_moments(gradient, moment, second, corr_one, corr_two):
    new_moment = BETA_ONE * moment + (1.0 - BETA_ONE) * gradient
    new_second = BETA_TWO * second + (1.0 - BETA_TWO) * gradient * gradient
    direction = new_moment / corr_one / (jnp.sqrt(new_second / corr_two) + ADAM_EPS)
    return (new_moment, new_second, direction)


def adamw(weight, gradient, moment, second, corr_one, corr_two, decay):
    new_moment, new_second, direction = adam_moments(gradient, moment, second, corr_one, corr_two)
    return (weight - LEARN_RATE * (direction + decay * weight), new_moment, new_second)


def matrix_of(stack, count, rows_in, cols_in):
    height = stack.shape[1]
    shaped = stack.reshape(count, rows_in, cols_in, height, BS)
    return shaped.transpose(1, 3, 0, 2, 4).reshape(rows_in, height, count * cols_in * BS)


def blocks_of(matrix, count, rows_in, cols_in):
    height = matrix.shape[1]
    shaped = matrix.reshape(rows_in, height, count, cols_in, BS)
    return shaped.transpose(2, 0, 3, 1, 4).reshape(count * rows_in * cols_in, height, BS)


def make_shards(sizes):
    size_f, size_g = sizes
    pieces = size_g // 2

    def shards(
        code_ids,
        mask_pos,
        mask_count,
        block_order,
        step_count,
        blocks,
        block_mom,
        block_var,
        rot_bases,
        embedding,
        embed_mom,
        embed_var,
        position,
        pos_mom,
        pos_var,
        head_w,
        head_mom,
        head_var,
        vectors,
        vec_mom,
        vec_var,
        out_bias,
        bias_mom,
        bias_var,
    ):
        index = (lax.axis_index("fsdp"), lax.axis_index("grp"))
        index_f, index_g = index
        seqs = code_ids.shape[0]
        width_f = embedding.shape[1]
        rows_f = blocks.shape[1]

        counted = jnp.full((8, 128), jnp.sum(mask_count), jnp.int32)
        for axis, size in (("fsdp", size_f), ("grp", size_g)):
            bit = 1
            while bit < size:
                counted = counted + swap(counted, axis, size, bit)
                bit *= 2
        masked_total = counted[0, 0].astype(F32)

        small = jnp.concatenate(
            [
                jnp.pad(embedding, ((0, VPAD - VOCAB), (0, 0))),
                position,
                head_w,
                jnp.pad(vectors, ((0, 32 - NVEC), (0, 0))),
            ],
            axis=0,
        )
        small = small.astype(BF).T
        low = blocks.astype(BF)
        mat_qkv = matrix_of(low[: 3 * SQ], 3, SIDE, SIDE)
        mat_o = matrix_of(low[3 * SQ : 4 * SQ], 1, SIDE, SIDE)
        mat_up = matrix_of(low[4 * SQ : 4 * SQ + SIDE * WIDE], 1, SIDE, WIDE)
        mat_down = matrix_of(low[4 * SQ + SIDE * WIDE :], 1, WIDE, SIDE)
        small = lax.all_gather(small, "fsdp", axis=0, tiled=True)
        w_att = lax.all_gather(jnp.concatenate([mat_qkv, mat_o], axis=2), "fsdp", axis=1, tiled=True)
        w_att = w_att.reshape(D, 4 * D)
        w_qkv = w_att[:, : 3 * D]
        w_o = w_att[:, 3 * D :]
        w_up = lax.all_gather(mat_up, "fsdp", axis=1, tiled=True).reshape(D, FF)
        w_down = lax.all_gather(mat_down, "fsdp", axis=1, tiled=True).reshape(FF, D)
        emb_t = small[:, :VPAD]
        pos = small[:, VPAD : VPAD + SEQ].T.astype(F32)
        head_t = small[:, VPAD + SEQ : VPAD + SEQ + D]
        vec = small[:, VPAD + SEQ + D :].T.astype(F32)
        gain_one, gain_two, gain_fin, gain_head = (1.0 + vec[i] for i in (0, 2, 4, 6))
        bias_one, bias_two, bias_fin, bias_head = (vec[i] for i in (1, 3, 5, 7))
        bias_qkv = jnp.concatenate([vec[8], jnp.zeros((D,), F32), vec[9]])
        bias_up = vec[13:17].reshape(FF)

        slot = jnp.arange(MASKN, dtype=jnp.int32)
        valid = slot[None, :] < mask_count[:, None]
        at_pos = mask_pos[:, :, None] == jnp.arange(SEQ, dtype=jnp.int32)[None, None, :]
        is_masked = jnp.any(at_pos & valid[:, :, None], axis=1)
        token_ids = jnp.where(is_masked, VOCAB - 1, code_ids).reshape(-1)
        targets = jnp.sum(jnp.where(at_pos, code_ids[:, None, :], 0), axis=2).reshape(-1)
        pick = at_pos.astype(BF)
        token_hot = (token_ids[:, None] == jnp.arange(VPAD, dtype=jnp.int32)[None, :]).astype(BF)

        x0 = mm(token_hot, emb_t, 1, 1)
        x0 = (x0.reshape(seqs, SEQ, D) + pos[None]).reshape(seqs * SEQ, D)
        hat_one, rstd_one = norm_parts(x0)
        act_a = (hat_one * gain_one + bias_one).astype(BF)
        qkv = (mm(act_a, w_qkv) + bias_qkv).astype(BF)
        mixed = attn_fwd(qkv)
        x1 = x0 + (mm(mixed, w_o) + vec[10])
        hat_two, rstd_two = norm_parts(x1)
        act_m = (hat_two * gain_two + bias_two).astype(BF)
        pre = mm(act_m, w_up) + bias_up
        act_h = (pre * gelu_cdf(pre)).astype(BF)
        x2 = x1 + (mm(act_h, w_down) + vec[11])
        hat_fin, rstd_fin = norm_parts(x2)
        final = (hat_fin * gain_fin + bias_fin).astype(BF).reshape(seqs, SEQ, D)
        picked = jnp.einsum("sjp,spd->sjd", pick, final, preferred_element_type=F32)
        picked = picked.reshape(seqs * MASKN, D).astype(BF)
        head_pre = mm(picked, head_t, 1, 1) + vec[12]
        hat_head, rstd_head = norm_parts(head_pre * gelu_cdf(head_pre))
        act_t = (hat_head * gain_head + bias_head).astype(BF)
        bias_pad = jnp.pad(out_bias, (0, VPAD - VOCAB), constant_values=-1e30)
        logits = mm(act_t, emb_t) + bias_pad
        slot_weight = valid.reshape(-1).astype(F32)
        log_norm = jax.nn.logsumexp(logits, axis=-1)
        hit = jnp.arange(VPAD, dtype=jnp.int32)[None, :] == targets[:, None]
        picked_logit = jnp.sum(jnp.where(hit, logits, 0.0), axis=-1)
        loss_part = jnp.sum(slot_weight * (log_norm - picked_logit)) / masked_total
        d_logits = (jnp.exp(logits - log_norm[:, None]) - hit.astype(F32)) * (slot_weight / masked_total)[:, None]
        d_logits = d_logits.astype(BF)
        grad_bias = col_total(d_logits)

        d_t = mm(d_logits, emb_t, 1, 1)
        grad_emb_out = mm(act_t, d_logits, 0, 0)
        d_gelu, grad_gain_head, grad_shift_head = norm_back(d_t, hat_head, rstd_head, gain_head)
        d_tp = (d_gelu * gelu_grad(head_pre)).astype(BF)
        grad_head = mm(d_tp, picked, 0, 0)
        chunk_head = jnp.concatenate([grad_head, grad_emb_out[:, CODES:]], axis=1)
        piece_head = reduce_chunk(chunk_head.reshape(1, size_f, width_f, -1), sizes, index)

        spread = jnp.einsum("sjp,sjd->spd", pick, d_tp.reshape(seqs, MASKN, D), preferred_element_type=F32)
        d_final = mm(spread.astype(BF).reshape(seqs * SEQ, D), head_t)
        d_x2, grad_gain_fin, grad_shift_fin = norm_back(d_final, hat_fin, rstd_fin, gain_fin)
        d_y = d_x2.astype(BF)
        grad_down = mm(act_h, d_y, 0, 0)
        piece_down = reduce_chunk(grad_down.reshape(WIDE, size_f, rows_f, D), sizes, index)
        d_u = (mm(d_y, w_down, 1, 1) * gelu_grad(pre)).astype(BF)
        grad_up = mm(act_m, d_u, 0, 0)
        piece_up = reduce_chunk(grad_up.reshape(SIDE, size_f, rows_f, FF), sizes, index)
        d_m = mm(d_u, w_up, 1, 1)
        d_norm, grad_gain_two, grad_shift_two = norm_back(d_m, hat_two, rstd_two, gain_two)
        d_x1 = d_x2 + d_norm
        d_att = d_x1.astype(BF)
        grad_o = mm(mixed, d_att, 0, 0)
        piece_o = reduce_chunk(grad_o.reshape(SIDE, size_f, rows_f, D), sizes, index)
        d_mixed = mm(d_att, w_o, 1, 1).astype(BF)
        d_qkv = attn_bwd(qkv, d_mixed)
        grad_qkv = mm(act_a, d_qkv, 0, 0)
        piece_qkv = reduce_chunk(grad_qkv.reshape(SIDE, size_f, rows_f, 3 * D), sizes, index)
        d_a = mm(d_qkv, w_qkv, 1, 1)
        d_norm, grad_gain_one, grad_shift_one = norm_back(d_a, hat_one, rstd_one, gain_one)
        d_x0 = d_x1 + d_norm
        grad_pos = jnp.sum(d_x0.reshape(seqs, SEQ, D), axis=0)
        high = d_x0.astype(BF)
        rest = (d_x0 - high.astype(F32)).astype(BF)
        codes_hot = token_hot[:, :CODES]
        grad_emb_low = grad_emb_out[:, :CODES] + mm(high, codes_hot, 0, 0) + mm(rest, codes_hot, 0, 0)
        masked_row = jnp.sum(jnp.where(is_masked.reshape(-1, 1), d_x0, 0.0), axis=0)
        sums_qkv = col_total(d_qkv)
        vec_rows = jnp.concatenate(
            [
                jnp.stack(
                    [
                        grad_gain_one,
                        grad_shift_one,
                        grad_gain_two,
                        grad_shift_two,
                        grad_gain_fin,
                        grad_shift_fin,
                        grad_gain_head,
                        grad_shift_head,
                        sums_qkv[:D],
                        sums_qkv[2 * D :],
                        col_total(d_att),
                        col_total(d_y),
                        col_total(d_tp),
                    ]
                ),
                col_total(d_u).reshape(FF // D, D),
                masked_row[None],
                jnp.pad(grad_bias, (0, 3 * D - VPAD)).reshape(3, D),
                jnp.zeros((128 - NVEC - 4, D), F32),
            ],
            axis=0,
        )
        chunk_last = jnp.concatenate([grad_emb_low, grad_pos.T, vec_rows.T], axis=1)
        piece_last = reduce_chunk(chunk_last.reshape(1, size_f, width_f, -1), sizes, index)

        late = CODES + SEQ
        piece_head = piece_head[0]
        piece_last = piece_last[0]
        at_mask = jnp.arange(piece_head.shape[1]) == D + VOCAB - 1 - CODES
        piece_head = piece_head + jnp.where(at_mask[None, :], piece_last[:, late + NVEC : late + NVEC + 1], 0.0)
        at_last = jnp.arange(piece_last.shape[1]) == late + NVEC
        piece_last = jnp.where(at_last[None, :], 0.0, piece_last)
        square_part = 0.0
        for item in (piece_head, piece_last, piece_down, piece_up, piece_o, piece_qkv):
            square_part = square_part + jnp.sum(item * item)
        share = piece_last.shape[0]
        piece_index = 0
        bit = 1
        while bit < size_g // 2:
            piece_index = piece_index * 2 + (index_g // bit) % 2
            bit *= 2
        row_at = index_f * width_f + piece_index * share
        bias_piece = piece_last[:, late + NVEC + 1 : late + NVEC + 4]
        bias_placed = lax.dynamic_update_slice(jnp.zeros((D, 3), F32), bias_piece * 0.5, (row_at, 0))
        scalars = jnp.stack([square_part * 0.5, loss_part])
        bias_sum, scalars = lax.psum((bias_placed, scalars), ("grp", "fsdp"))
        loss_out = scalars[1]
        clip_norm = jnp.sqrt(scalars[0])
        clip_scale = CLIP_LEVEL / jnp.maximum(clip_norm, CLIP_LEVEL)
        step_float = step_count.astype(F32)
        corr_one = 1.0 - jnp.power(BETA_ONE, step_float)
        corr_two = 1.0 - jnp.power(BETA_TWO, step_float)
        send_scale = clip_scale * CLIP_UP

        natural = jnp.concatenate(
            [
                blocks_of(piece_qkv, 3, SIDE, SIDE),
                blocks_of(piece_o, 1, SIDE, SIDE),
                blocks_of(piece_up, 1, SIDE, WIDE),
                blocks_of(piece_down, 1, WIDE, SIDE),
            ],
            axis=0,
        )
        natural = (natural * send_scale).astype(F16)
        owned_count = NB // size_f
        cut = natural.shape[1]
        permuted = jnp.take(natural, block_order, axis=0).reshape(size_f, owned_count, cut, BS)
        owned = lax.all_to_all(permuted, "fsdp", split_axis=0, concat_axis=0, tiled=True)
        owned = gather_rows(owned.reshape(size_f * owned_count, cut, BS), size_g, index_g)
        owned = owned.reshape(size_f, owned_count, rows_f, BS).transpose(1, 0, 2, 3).reshape(owned_count, BS, BS)
        owned = owned.astype(F32) * (1.0 / CLIP_UP)

        both = jnp.concatenate([piece_head, piece_last], axis=1)
        both = gather_rows((both * send_scale).astype(F16)[None], size_g, index_g)[0]
        both = both.astype(F32).T * (1.0 / CLIP_UP)
        clip_head = both[:D]
        split = D + CODES
        clip_emb = jnp.concatenate([both[split : split + CODES], both[D : D + VOCAB - CODES]], axis=0)
        clip_pos = both[split + CODES : split + CODES + SEQ]
        clip_vec = both[split + CODES + SEQ : split + CODES + SEQ + NVEC]
        clip_bias = bias_sum.T.reshape(3 * D)[:VOCAB] * clip_scale

        left = rot_bases[:, 0]
        right = rot_bases[:, 1]
        prec = lax.Precision.HIGH
        rotated = jnp.einsum("sji,sjk->sik", left, owned, precision=prec)
        rotated = jnp.einsum("sik,skl->sil", rotated, right, precision=prec)
        new_block_mom, new_block_var, direction = adam_moments(rotated, block_mom, block_var, corr_one, corr_two)
        turned = jnp.einsum("sij,sjk->sik", left, direction, precision=prec)
        slot_update = jnp.einsum("sik,slk->sil", turned, right, precision=prec).astype(F16)
        received = lax.all_to_all(slot_update, "fsdp", split_axis=1, concat_axis=0, tiled=True)
        block_index = jnp.arange(NB, dtype=jnp.int32)
        inverse = jnp.sum(
            jnp.where(block_order[None, :] == block_index[:, None], block_index[None, :], 0), axis=1
        )
        update = jnp.take(received, inverse, axis=0).astype(F32)
        new_blocks = blocks - LEARN_RATE * (update + DECAY_RATE * blocks)
        new_embedding, new_embed_mom, new_embed_var = adamw(
            embedding, clip_emb, embed_mom, embed_var, corr_one, corr_two, DECAY_RATE
        )
        new_position, new_pos_mom, new_pos_var = adamw(
            position, clip_pos, pos_mom, pos_var, corr_one, corr_two, DECAY_RATE
        )
        new_head_w, new_head_mom, new_head_var = adamw(
            head_w, clip_head, head_mom, head_var, corr_one, corr_two, DECAY_RATE
        )
        new_vectors, new_vec_mom, new_vec_var = adamw(
            vectors, clip_vec, vec_mom, vec_var, corr_one, corr_two, 0.0
        )
        new_out_bias, new_bias_mom, new_bias_var = adamw(
            out_bias, clip_bias, bias_mom, bias_var, corr_one, corr_two, 0.0
        )
        return (
            loss_out,
            clip_norm,
            new_blocks,
            new_block_mom,
            new_block_var,
            new_embedding,
            new_embed_mom,
            new_embed_var,
            new_position,
            new_pos_mom,
            new_pos_var,
            new_head_w,
            new_head_mom,
            new_head_var,
            new_vectors,
            new_vec_mom,
            new_vec_var,
            new_out_bias,
            new_bias_mom,
            new_bias_var,
        )

    return shards


def solution(mesh):
    sizes = (mesh.shape["fsdp"], mesh.shape["grp"])
    wide = P(None, "fsdp")
    placed = (
        P(("grp", "fsdp"), None),
        P(("grp", "fsdp"), None),
        P(("grp", "fsdp")),
        P(),
        P(),
        P(None, "fsdp", None),
        P("fsdp", None, None),
        P("fsdp", None, None),
        P("fsdp", None, None, None),
        *([wide] * 12),
        P(),
        P(),
        P(),
    )
    return jax.shard_map(
        make_shards(sizes),
        mesh=mesh,
        in_specs=placed,
        out_specs=(
            P(),
            P(),
            P(None, "fsdp", None),
            P("fsdp", None, None),
            P("fsdp", None, None),
            *([wide] * 12),
            P(),
            P(),
            P(),
        ),
        check_vma=False,
    )
```
